512 devices in a mesh: grp: 16 (over z, core), seq: 32 (over y, x).
Axes of the slice: x: 4, y: 8, z: 8, core: 2. Of those that a mesh axis runs over, the one named last changes fastest.
Arguments:
- queries: bfloat16 [65536, 4096], P(('seq', 'grp')), may hold values from -6 to 6
- keys: bfloat16 [65536, 4096], P(('seq', 'grp')), may hold values from -6 to 6
- values: bfloat16 [65536, 4096], P(('seq', 'grp')), may hold values from -6 to 6
- log_decay: float32 [32, 65536], P('grp', 'seq'), may hold values from -1.3 to 0, as said below
- gain: float32 [4096], P('grp'), may hold values from 0.5 to 1.5
Outputs:
- attended: bfloat16 [65536, 4096], P('seq', 'grp')
The draws below stay inside these ranges and needn't reach their ends.
Inputs may be any that keep to these rules, and one draw needn't show every extreme that they name: log_decay is negative everywhere.
All inputs are finite; a program needn't handle non-finite values.
Results may differ from the reference program's by a relative error of at most 0.0059.
Values may be sent and summed in bfloat16 or wider, within the bound.
A program may use at most 64 MiB of HBM per device.

```python
import math
import jax
import jax.numpy as jnp
from jax import lax

HEAD_TOTAL = 32
HEAD_DIM = 128
T_DEV = 2048
TOKEN_TOTAL = 65536


def draw_log_decay(key, part):
    every_key = jax.random.split(jax.random.fold_in(key, 17), 6)
    block_count = TOKEN_TOTAL // T_DEV
    slow_share = 0.5
    slow_heads = jax.random.uniform(every_key[0], (HEAD_TOTAL, 1)) < slow_share
    slow_rates = jnp.exp(jax.random.uniform(every_key[1], (HEAD_TOTAL, 1), minval=math.log(0.1), maxval=math.log(0.5))) / TOKEN_TOTAL
    fast_rates = jnp.exp(jax.random.uniform(every_key[2], (HEAD_TOTAL, 1), minval=math.log(1.0 / 50.0), maxval=math.log(1.0 / 30.0)))
    base_rates = jnp.where(slow_heads, slow_rates, fast_rates)
    factor = jnp.exp(jax.random.uniform(every_key[3], (HEAD_TOTAL, block_count), minval=math.log(0.5), maxval=math.log(2.0)))
    rates = base_rates * jnp.repeat(factor, T_DEV, axis=1)
    spike_location = jax.random.randint(every_key[4], (3,), 0, TOKEN_TOTAL)
    spike_penalty = jax.random.uniform(every_key[5], (HEAD_TOTAL, 3), minval=0.2, maxval=0.33)
    position_index = jnp.arange(TOKEN_TOTAL)
    final_output = -rates
    for selected_index in range(3):
        spike_mask = (position_index == spike_location[selected_index]).astype(jnp.float32)
        final_output = final_output + jnp.log1p(-spike_penalty[:, selected_index:selected_index + 1]) * spike_mask[None, :]
    return final_output.astype(jnp.float32)


def level_of(own_key, dims, shards, least, largest):
    factor_of, own = 1.0, jax.random.fold_in(own_key, 6)
    for dim, blocks in shards:
        steps = jnp.exp(jax.random.uniform(jax.random.fold_in(own, dim), (blocks,), jnp.float32, least / len(shards), largest / len(shards)))
        factor_of = factor_of * jnp.repeat(steps, dims[dim] // blocks).reshape([-1 if axis == dim else 1 for axis in range(len(dims))])
    return factor_of


def gaussian(stream_key, extent, width, limit, shards=(), held_as=jnp.bfloat16):
    drawn = jax.random.normal(stream_key, extent, jnp.float32) * width
    if len(shards) > 0:
        drawn = level_of(stream_key, extent, shards, -0.22, 0.18) * drawn
    return jnp.clip(drawn, min=-limit, max=limit).astype(held_as)


def setup_inputs(seed: int = 0) -> dict:
    seeds = jax.random.split(jax.random.key(seed), 6)
    return {
        "queries": gaussian(seeds[0], (TOKEN_TOTAL, HEAD_TOTAL * HEAD_DIM), 1.0, 6.0, ((0, 512),)),
        "keys": gaussian(seeds[1], (TOKEN_TOTAL, HEAD_TOTAL * HEAD_DIM), 1.0, 6.0, ((0, 512),)),
        "values": gaussian(seeds[2], (TOKEN_TOTAL, HEAD_TOTAL * HEAD_DIM), 1.0, 6.0, ((0, 512),)),
        "log_decay": draw_log_decay(jax.random.fold_in(seeds[5], 71), 0),
        "gain": jnp.clip(1.0 + 0.1 * jax.random.normal(seeds[4], (HEAD_TOTAL * HEAD_DIM,), jnp.float32), 0.5, 1.5),
    }


def local_mix(query_part, key_part, value_part, levels):
    highest = lax.Precision.HIGHEST
    row_total = query_part.shape[0]
    block_rows = min(512, row_total)
    pieces = []
    for start in range(0, row_total, block_rows):
        finish = start + block_rows
        scores = jnp.einsum('thd,shd->hts', query_part[start:finish], key_part[:finish], precision=highest)
        causal = jnp.arange(start, finish, dtype=jnp.int32)[:, None] >= jnp.arange(finish, dtype=jnp.int32)[None, :]
        decay_gap = jnp.where(causal[None], levels[:, start:finish, None] - levels[:, None, :finish], 0.0)
        weights = jnp.where(causal[None], scores * jnp.exp(decay_gap), 0.0).astype(jnp.bfloat16)
        weights = lax.optimization_barrier(weights)
        pieces.append(jnp.einsum('hts,shd->thd', weights.astype(jnp.float32), value_part[:finish], precision=highest))
    return jnp.concatenate(pieces, axis=0)

def reference(queries, keys, values, log_decay, gain):
    total_rows = queries.shape[0]
    block_count = total_rows // T_DEV
    query_blocks = queries.reshape(block_count, T_DEV, HEAD_TOTAL, HEAD_DIM)
    key_blocks = keys.reshape(block_count, T_DEV, HEAD_TOTAL, HEAD_DIM)
    value_blocks = values.reshape(block_count, T_DEV, HEAD_TOTAL, HEAD_DIM)
    decay_blocks = log_decay.reshape(HEAD_TOTAL, block_count, T_DEV).transpose(1, 0, 2)
    gain_heads = gain.reshape(HEAD_TOTAL, HEAD_DIM)
    highest = lax.Precision.HIGHEST

    def advance(running_state, inputs):
        query_part, key_part, value_part, decay_part = inputs
        query_wide = query_part.astype(jnp.float32)
        key_wide = key_part.astype(jnp.float32)
        value_wide = value_part.astype(jnp.float32)
        levels = jnp.cumsum(decay_part, axis=1)
        block_total = levels[:, -1]
        local_part = local_mix(query_wide, key_wide, value_wide, levels)
        state_half = lax.optimization_barrier(running_state.astype(jnp.bfloat16))
        scaled_queries = (query_wide * jnp.exp(levels).T[:, :, None]).astype(jnp.bfloat16)
        scaled_queries = lax.optimization_barrier(scaled_queries)
        carried_part = jnp.einsum('thd,hde->the', scaled_queries.astype(jnp.float32), state_half.astype(jnp.float32), precision=highest)
        mixture = local_part + carried_part
        mean_square = lax.optimization_barrier(jnp.mean(mixture * mixture, axis=2, keepdims=True))
        normed = (mixture * lax.rsqrt(mean_square + 1e-06) * gain_heads[None]).astype(jnp.bfloat16)
        tail_decay = jnp.exp(block_total[:, None] - levels)
        scaled_keys = (key_wide * tail_decay.T[:, :, None]).astype(jnp.bfloat16)
        scaled_keys = lax.optimization_barrier(scaled_keys)
        block_state = jnp.einsum('thd,the->hde', scaled_keys.astype(jnp.float32), value_wide, precision=highest)
        next_state = jnp.exp(block_total)[:, None, None] * running_state + block_state
        return (next_state, normed)
    starting = jnp.zeros((HEAD_TOTAL, HEAD_DIM, HEAD_DIM), jnp.float32)
    _, outputs = lax.scan(advance, starting, (query_blocks, key_blocks, value_blocks, decay_blocks))
    return outputs.reshape(total_rows, HEAD_TOTAL * HEAD_DIM)
```

```python
import functools

import jax
import jax.numpy as jnp
from jax import lax
from jax.experimental import pallas as pl
from jax.experimental.pallas import tpu as pltpu
from jax.sharding import PartitionSpec as P

MESH = pl.DeviceIdType.MESH
F32 = jnp.float32
BF16 = jnp.bfloat16
CHIPS = 8
GROUP = 16
ROWS = 128
WIDTH = 128
X_SIZE = 4
Y_SIZE = 8


def order(i):
    m = i // 2
    odd = m % 2
    return 4 + (1 - 2 * odd) * ((m + 1) // 2), 1 - i % 2


def kernel(
    q_hbm, k_hbm, v_hbm, decay_ref, gain_ref, out_hbm,
    q_own, k_own, v_own, level, total, level_out, level_in,
    q_in, state_own, state_sib, state_out, state_in, local_out, local_in,
    block_out, x_state, x_total, row_out, y_state, y_total, tot_out, rowtot_out,
    entering, prefix, carried, result,
    load_sem, level_s, level_r, q_s, q_r, sib_s, sib_r, state_s, state_r, local_s, local_r,
    x_s, x_r, xt_s, xt_r, y_s, y_r, yt_s, yt_r, out_sem,
):
    g = lax.axis_index("grp")
    s = lax.axis_index("seq")
    z, c = g // 2, lax.rem(g, 2)
    y, x = s // X_SIZE, lax.rem(s, X_SIZE)
    cf = c.astype(F32)
    sibling = g + 1 - 2 * c

    def peer(i):
        dz, dc = order(i)
        return lax.rem(z + dz, CHIPS) * 2 + lax.rem(c + dc, 2)

    def source(i):
        dz, dc = order(i)
        return lax.rem(z + 2 * CHIPS - dz, CHIPS) * 2 + lax.rem(c + dc, 2)

    def cols(p):
        return pl.ds(pl.multiple_of(p * 2 * WIDTH, 2 * WIDTH), 2 * WIDTH)

    loads = [
        pltpu.make_async_copy(k_hbm, k_own, load_sem.at[0]),
        pltpu.make_async_copy(v_hbm, v_own, load_sem.at[1]),
        pltpu.make_async_copy(q_hbm, q_own, load_sem.at[2]),
        pltpu.make_async_copy(q_hbm.at[:, cols(g)], q_in.at[g], load_sem.at[3]),
    ]
    for copy in loads:
        copy.start()

    barrier = pltpu.get_barrier_semaphore()
    peers = [peer(i) for i in range(GROUP - 1)]
    row_mates = [y * X_SIZE + lax.rem(x + d, X_SIZE) for d in range(1, X_SIZE)]
    column_mates = [lax.rem(y + d, Y_SIZE) * X_SIZE + x for d in range(1, Y_SIZE)]
    for p in peers:
        pl.semaphore_signal(barrier, inc=1, device_id=(p, s), device_id_type=MESH)
    for m in row_mates + column_mates:
        pl.semaphore_signal(barrier, inc=1, device_id=(g, m), device_id_type=MESH)

    here = lax.broadcasted_iota(jnp.int32, (ROWS, ROWS), 0)
    there = lax.broadcasted_iota(jnp.int32, (ROWS, ROWS), 1)
    upto = (here <= there).astype(F32)
    chunk_levels = jnp.dot(
        decay_ref[...], upto, preferred_element_type=F32, precision=lax.Precision.HIGHEST
    )
    chunk_totals = jnp.broadcast_to(chunk_levels[:, ROWS - 1 : ROWS], (2 * GROUP, ROWS))
    level[...] = chunk_levels
    total[...] = chunk_totals
    for n in range(CHIPS):
        level_out[n, 0:4, :] = chunk_levels[4 * n : 4 * n + 4]
        level_out[n, 4:8, :] = chunk_levels[4 * n : 4 * n + 4]
    for h in range(2):
        block_total = chunk_totals[h : h + 1]
        for n in range(1, GROUP):
            block_total = block_total + chunk_totals[2 * n + h : 2 * n + h + 1]
        tot_out[4 * h : 4 * h + 4, :] = jnp.broadcast_to(block_total, (4, ROWS))
    level_in[g] = level_out[z]
    x_total[x] = tot_out[...]

    pl.semaphore_wait(barrier, len(peers) + len(row_mates) + len(column_mates))

    def level_copy(p, slot):
        return pltpu.make_async_remote_copy(
            src_ref=level_out.at[p // 2], dst_ref=level_in.at[slot],
            send_sem=level_s.at[p], recv_sem=level_r.at[slot],
            device_id=(p, s), device_id_type=MESH,
        )

    def q_copy(p, slot):
        return pltpu.make_async_remote_copy(
            src_ref=q_hbm.at[:, cols(p)], dst_ref=q_in.at[slot],
            send_sem=q_s.at[p], recv_sem=q_r.at[slot],
            device_id=(p, s), device_id_type=MESH,
        )

    def sib_copy(p):
        return pltpu.make_async_remote_copy(
            src_ref=state_own.at[p], dst_ref=state_sib.at[p],
            send_sem=sib_s.at[p], recv_sem=sib_r.at[p],
            device_id=(sibling, s), device_id_type=MESH,
        )

    def state_copy(chip, slot):
        return pltpu.make_async_remote_copy(
            src_ref=state_out.at[chip], dst_ref=state_in.at[slot],
            send_sem=state_s.at[chip], recv_sem=state_r.at[slot],
            device_id=(chip * 2 + c, s), device_id_type=MESH,
        )

    def local_copy(p, slot):
        return pltpu.make_async_remote_copy(
            src_ref=local_out.at[p], dst_ref=local_in.at[slot],
            send_sem=local_s.at[p], recv_sem=local_r.at[slot],
            device_id=(p, s), device_id_type=MESH,
        )

    def x_copy(d, slot):
        return pltpu.make_async_remote_copy(
            src_ref=block_out, dst_ref=x_state.at[slot],
            send_sem=x_s.at[d], recv_sem=x_r.at[slot],
            device_id=(g, row_mates[d]), device_id_type=MESH,
        )

    def xt_copy(d, slot):
        return pltpu.make_async_remote_copy(
            src_ref=tot_out, dst_ref=x_total.at[slot],
            send_sem=xt_s.at[d], recv_sem=xt_r.at[slot],
            device_id=(g, row_mates[d]), device_id_type=MESH,
        )

    def y_copy(d, slot):
        return pltpu.make_async_remote_copy(
            src_ref=row_out, dst_ref=y_state.at[slot],
            send_sem=y_s.at[d], recv_sem=y_r.at[slot],
            device_id=(g, column_mates[d]), device_id_type=MESH,
        )

    def yt_copy(d, slot):
        return pltpu.make_async_remote_copy(
            src_ref=rowtot_out, dst_ref=y_total.at[slot],
            send_sem=yt_s.at[d], recv_sem=yt_r.at[slot],
            device_id=(g, column_mates[d]), device_id_type=MESH,
        )

    for p in peers:
        level_copy(p, g).start()
    for d in range(X_SIZE - 1):
        xt_copy(d, x).start()
    for p in peers:
        q_copy(p, g).start()

    for copy in loads:
        copy.wait()

    @pl.loop(0, GROUP - 1)
    def _(i):
        p = source(i)
        level_copy(p, p).wait_recv()

    def spread(row):
        wide = jnp.broadcast_to(row, (ROWS, ROWS))
        return wide, wide.T

    def head_cols(p, h):
        return pl.ds(pl.multiple_of(p * 2 * WIDTH + h * WIDTH, WIDTH), WIDTH)

    @pl.loop(0, GROUP)
    def _(i):
        p = peer(i)
        for h in range(2):
            _, down = spread(level_in[p, pl.ds(2 * c + h, 1), :])
            tail = jnp.exp(down[ROWS - 1 : ROWS, :] - down)
            scaled = (k_own[:, head_cols(p, h)].astype(F32) * tail).astype(BF16)
            state_own[p, h] = lax.dot_general(
                scaled, v_own[:, head_cols(p, h)], (((0,), (0,)), ((), ())),
                preferred_element_type=F32,
            )
        sib_copy(p).start()

    @pl.loop(0, GROUP)
    def _(i):
        p = peer(i)
        sib_copy(p).wait_recv()

        @pl.when(lax.rem(p, 2) == c)
        def _():
            for h in range(2):
                late = jnp.broadcast_to(level_in[p, 2 + h : 3 + h, ROWS - 1 : ROWS], (1, WIDTH))
                merged = (
                    jnp.exp(late * (1.0 - cf)) * state_own[p, h]
                    + jnp.exp(late * cf) * state_sib[p, h]
                )
                state_out[p // 2, h] = merged.astype(BF16)

            @pl.when(i < GROUP - 1)
            def _():
                state_copy(p // 2, z).start()

            @pl.when(i == GROUP - 1)
            def _():
                state_in[z] = state_out[z]

    causal = here >= there

    @pl.loop(0, GROUP)
    def _(i):
        p = peer(i)
        for h in range(2):
            wide, down = spread(level_in[p, pl.ds(2 * c + h, 1), :])
            q_head = q_own[:, head_cols(p, h)]
            scores = lax.dot_general(
                q_head, k_own[:, head_cols(p, h)], (((1,), (1,)), ((), ())),
                preferred_element_type=F32,
            )
            gap = jnp.where(causal, down - wide, 0.0)
            weights = jnp.where(causal, scores * jnp.exp(gap), 0.0).astype(BF16)
            part = jnp.dot(weights, v_own[:, head_cols(p, h)], preferred_element_type=F32)
            scaled = (q_head.astype(F32) * (jnp.exp(down) * cf)).astype(BF16)
            part = part + jnp.dot(
                scaled, state_sib[p, h].astype(BF16), preferred_element_type=F32
            )
            local_out[p, :, h * WIDTH : (h + 1) * WIDTH] = part.astype(BF16)

        @pl.when(i < GROUP - 1)
        def _():
            local_copy(p, g).start()

        @pl.when(i == GROUP - 1)
        def _():
            local_in[g] = local_out[g]

    @pl.loop(1, CHIPS)
    def _(d):
        chip = lax.rem(z + d, CHIPS)
        state_copy(chip, chip).wait_recv()

    def chip_share(n, h):
        return jnp.exp(total[4 * n + h : 4 * n + h + 1, :] + total[4 * n + 2 + h : 4 * n + 3 + h, :])

    for h in range(2):
        run = state_in[0, h].astype(F32)
        for n in range(1, CHIPS):
            run = chip_share(n, h) * run + state_in[n, h].astype(F32)
        block_out[h] = run.astype(BF16)
    for d in range(X_SIZE - 1):
        x_copy(d, x).start()
    x_state[x] = block_out[...]
    for d in range(1, X_SIZE):
        mate = lax.rem(x + d, X_SIZE)
        x_copy(d - 1, mate).wait_recv()
        xt_copy(d - 1, mate).wait_recv()

    for h in range(2):
        run = x_state[0, h].astype(F32)
        row_total = x_total[0, 4 * h : 4 * h + 1, :]
        for n in range(1, X_SIZE):
            here_total = x_total[n, 4 * h : 4 * h + 1, :]
            run = jnp.exp(here_total) * run + x_state[n, h].astype(F32)
            row_total = row_total + here_total
        row_out[h] = run.astype(BF16)
        rowtot_out[4 * h : 4 * h + 4, :] = jnp.broadcast_to(row_total, (4, ROWS))
    for d in range(Y_SIZE - 1):
        yt_copy(d, y).start()
        y_copy(d, y).start()
    y_state[y] = row_out[...]
    y_total[y] = rowtot_out[...]
    for d in range(1, Y_SIZE):
        mate = lax.rem(y + d, Y_SIZE)
        y_copy(d - 1, mate).wait_recv()
        yt_copy(d - 1, mate).wait_recv()

    for h in range(2):
        run = jnp.zeros((WIDTH, WIDTH), F32)
        for n in range(Y_SIZE - 1):
            used = (n < y).astype(F32)
            run = jnp.exp(y_total[n, 4 * h : 4 * h + 1, :] * used) * run + (
                y_state[n, h].astype(F32) * used
            )
        for n in range(X_SIZE - 1):
            used = (n < x).astype(F32)
            run = jnp.exp(x_total[n, 4 * h : 4 * h + 1, :] * used) * run + (
                x_state[n, h].astype(F32) * used
            )
        for n in range(CHIPS):
            prefix[n, h] = run.astype(BF16)
            run = chip_share(n, h) * run + state_in[n, h].astype(F32)

    @pl.loop(0, GROUP - 1)
    def _(i):
        p = source(i)
        q_copy(p, p).wait_recv()

    @pl.loop(0, GROUP)
    def _(p):
        chip, core = p // 2, lax.rem(p, 2)
        for h in range(2):
            row = level[pl.ds(2 * p + h, 1), :] + core.astype(F32) * total[pl.ds(4 * chip + h, 1), :]
            _, down = spread(row)
            scaled = (q_in[p, :, h * WIDTH : (h + 1) * WIDTH].astype(F32) * jnp.exp(down)).astype(BF16)
            carried[p, :, h * WIDTH : (h + 1) * WIDTH] = jnp.dot(
                scaled, prefix[chip, h], preferred_element_type=F32
            )

    def out_copy(p):
        return pltpu.make_async_copy(
            result.at[p], out_hbm.at[pl.ds(pl.multiple_of(p * ROWS, ROWS), ROWS), :], out_sem.at[p]
        )

    def finish(p):
        for h in range(2):
            part = slice(h * WIDTH, (h + 1) * WIDTH)
            mixture = carried[p, :, part] + local_in[p, :, part].astype(F32)
            mean_square = jnp.mean(mixture * mixture, axis=1, keepdims=True)
            normed = mixture * lax.rsqrt(mean_square + 1e-06) * gain_ref[:, part]
            result[p, :, part] = normed.astype(BF16)
        out_copy(p).start()

    finish(g)

    @pl.loop(0, GROUP - 1)
    def _(i):
        p = source(i)
        local_copy(p, p).wait_recv()
        finish(p)

    @pl.loop(0, GROUP)
    def _(p):
        out_copy(p).wait()
        sib_copy(p).wait_send()

    @pl.loop(0, GROUP - 1)
    def _(i):
        p = peer(i)
        level_copy(p, g).wait_send()
        q_copy(p, g).wait_send()
        local_copy(p, g).wait_send()

    @pl.loop(1, CHIPS)
    def _(d):
        state_copy(lax.rem(z + d, CHIPS), z).wait_send()

    for d in range(X_SIZE - 1):
        x_copy(d, x).wait_send()
        xt_copy(d, x).wait_send()
    for d in range(Y_SIZE - 1):
        y_copy(d, y).wait_send()
        yt_copy(d, y).wait_send()


def local(queries, keys, values, log_decay, gain):
    chunk_decay = log_decay.reshape(2, GROUP, ROWS).transpose(1, 0, 2).reshape(2 * GROUP, ROWS)
    any_space = pl.BlockSpec(memory_space=pl.ANY)
    vmem = pl.BlockSpec(memory_space=pltpu.VMEM)
    dma = pltpu.SemaphoreType.DMA
    own = pltpu.VMEM((ROWS, GROUP * 2 * WIDTH), BF16)
    tile = pltpu.VMEM((8, ROWS), F32)
    return pl.pallas_call(
        kernel,
        out_shape=jax.ShapeDtypeStruct((GROUP * ROWS, 2 * WIDTH), BF16),
        in_specs=[any_space, any_space, any_space, vmem, vmem],
        out_specs=any_space,
        scratch_shapes=[
            own, own, own,
            pltpu.VMEM((2 * GROUP, ROWS), F32),
            pltpu.VMEM((2 * GROUP, ROWS), F32),
            pltpu.VMEM((CHIPS, 8, ROWS), F32),
            pltpu.VMEM((GROUP, 8, ROWS), F32),
            pltpu.VMEM((GROUP, ROWS, 2 * WIDTH), BF16),
            pltpu.VMEM((GROUP, 2, WIDTH, WIDTH), F32),
            pltpu.VMEM((GROUP, 2, WIDTH, WIDTH), F32),
            pltpu.VMEM((CHIPS, 2, WIDTH, WIDTH), BF16),
            pltpu.VMEM((CHIPS, 2, WIDTH, WIDTH), BF16),
            pltpu.VMEM((GROUP, ROWS, 2 * WIDTH), BF16),
            pltpu.VMEM((GROUP, ROWS, 2 * WIDTH), BF16),
            pltpu.VMEM((2, WIDTH, WIDTH), BF16),
            pltpu.VMEM((X_SIZE, 2, WIDTH, WIDTH), BF16),
            pltpu.VMEM((X_SIZE, 8, ROWS), F32),
            pltpu.VMEM((2, WIDTH, WIDTH), BF16),
            pltpu.VMEM((Y_SIZE, 2, WIDTH, WIDTH), BF16),
            pltpu.VMEM((Y_SIZE, 8, ROWS), F32),
            tile, tile,
            pltpu.VMEM((2, WIDTH, WIDTH), F32),
            pltpu.VMEM((CHIPS, 2, WIDTH, WIDTH), BF16),
            pltpu.VMEM((GROUP, ROWS, 2 * WIDTH), F32),
            pltpu.VMEM((GROUP, ROWS, 2 * WIDTH), BF16),
            dma((4,)),
            dma((GROUP,)), dma((GROUP,)),
            dma((GROUP,)), dma((GROUP,)),
            dma((GROUP,)), dma((GROUP,)),
            dma((CHIPS,)), dma((CHIPS,)),
            dma((GROUP,)), dma((GROUP,)),
            dma((X_SIZE,)), dma((X_SIZE,)), dma((X_SIZE,)), dma((X_SIZE,)),
            dma((Y_SIZE,)), dma((Y_SIZE,)), dma((Y_SIZE,)), dma((Y_SIZE,)),
            dma((GROUP,)),
        ],
        compiler_params=pltpu.CompilerParams(
            collective_id=0, has_side_effects=True, vmem_limit_bytes=60 << 20
        ),
    )(queries, keys, values, chunk_decay, gain.reshape(1, 2 * WIDTH))


def solution(mesh):
    return jax.shard_map(
        local,
        mesh=mesh,
        in_specs=(
            P(("seq", "grp"), None), P(("seq", "grp"), None), P(("seq", "grp"), None),
            P("grp", "seq"), P("grp"),
        ),
        out_specs=P("seq", "grp"),
        check_vma=False,
    )
```

```python
import functools

import jax
import jax.numpy as jnp
from jax import lax
from jax.experimental import pallas as pl
from jax.experimental.pallas import tpu as pltpu
from jax.sharding import PartitionSpec as P

MESH = pl.DeviceIdType.MESH
F32 = jnp.float32
BF16 = jnp.bfloat16
CHIPS = 8
GROUP = 16
ROWS = 128
WIDTH = 128
X_SIZE = 4
Y_SIZE = 8


def order(i):
    m = i // 2
    odd = m % 2
    return 4 + (1 - 2 * odd) * ((m + 1) // 2), 1 - i % 2


def kernel(
    q_hbm, k_hbm, v_hbm, decay_hbm, gain_hbm, out_hbm,
    decay_ref, gain_ref,
    q_own, k_own, v_own, level, total, level_out, level_in,
    q_in, state_own, state_sib, state_out, state_in, local_out, local_in,
    block_out, x_state, x_total, row_out, y_state, y_total, tot_out, rowtot_out,
    prefix, carried, result,
    load_sem, level_s, level_r, q_s, q_r, sib_s, sib_r, state_s, state_r, local_s, local_r,
    x_s, x_r, xt_s, xt_r, y_s, y_r, yt_s, yt_r, out_sem, gate,
):
    g = lax.axis_index("grp")
    s = lax.axis_index("seq")
    z, c = g // 2, lax.rem(g, 2)
    y, x = s // X_SIZE, lax.rem(s, X_SIZE)
    cf = c.astype(F32)
    sibling = g + 1 - 2 * c

    def peer(i):
        dz, dc = order(i)
        return lax.rem(z + dz, CHIPS) * 2 + lax.rem(c + dc, 2)

    def source(i):
        dz, dc = order(i)
        return lax.rem(z + 2 * CHIPS - dz, CHIPS) * 2 + lax.rem(c + dc, 2)

    def cols(p):
        return pl.ds(pl.multiple_of(p * 2 * WIDTH, 2 * WIDTH), 2 * WIDTH)

    barrier = pltpu.get_barrier_semaphore()
    peers = [peer(i) for i in range(GROUP - 1)]
    row_mates = [y * X_SIZE + lax.rem(x + d, X_SIZE) for d in range(1, X_SIZE)]
    column_mates = [lax.rem(y + d, Y_SIZE) * X_SIZE + x for d in range(1, Y_SIZE)]
    same_core = [lax.rem(z + d, CHIPS) * 2 + c for d in (4, 3, 5, 2, 6, 1, 7)]
    for p in same_core:
        pl.semaphore_signal(barrier, inc=1, device_id=(p, s), device_id_type=MESH)

    @pl.when(c == 1)
    def _():
        for n in range(CHIPS):
            pl.semaphore_signal(barrier, inc=1, device_id=(2 * n, s), device_id_type=MESH)

    for m in row_mates + column_mates:
        pl.semaphore_signal(barrier, inc=1, device_id=(g, m), device_id_type=MESH)

    decay_load = pltpu.make_async_copy(decay_hbm, decay_ref, load_sem.at[4])
    decay_load.start()
    loads = [
        pltpu.make_async_copy(k_hbm, k_own, load_sem.at[0]),
        pltpu.make_async_copy(v_hbm, v_own, load_sem.at[1]),
        pltpu.make_async_copy(q_hbm, q_own, load_sem.at[2]),
        pltpu.make_async_copy(q_hbm.at[:, cols(g)], q_in.at[g], load_sem.at[3]),
        pltpu.make_async_copy(gain_hbm, gain_ref, load_sem.at[5]),
    ]
    for copy in loads:
        copy.start()

    def level_copy(p, slot):
        return pltpu.make_async_remote_copy(
            src_ref=level_out.at[p // 2], dst_ref=level_in.at[slot],
            send_sem=level_s.at[p], recv_sem=level_r.at[slot],
            device_id=(p, s), device_id_type=MESH,
        )

    def q_copy(p, slot):
        return pltpu.make_async_remote_copy(
            src_ref=q_hbm.at[:, cols(p)], dst_ref=q_in.at[slot],
            send_sem=q_s.at[p], recv_sem=q_r.at[slot],
            device_id=(p, s), device_id_type=MESH,
        )

    def sib_copy(p):
        return pltpu.make_async_remote_copy(
            src_ref=state_own.at[p], dst_ref=state_sib.at[p],
            send_sem=sib_s.at[p], recv_sem=sib_r.at[p],
            device_id=(sibling, s), device_id_type=MESH,
        )

    def state_copy(chip, slot):
        return pltpu.make_async_remote_copy(
            src_ref=state_out.at[chip], dst_ref=state_in.at[slot],
            send_sem=state_s.at[chip], recv_sem=state_r.at[slot],
            device_id=(chip * 2 + c, s), device_id_type=MESH,
        )

    def local_copy(p, slot):
        return pltpu.make_async_remote_copy(
            src_ref=local_out.at[p], dst_ref=local_in.at[slot],
            send_sem=local_s.at[p], recv_sem=local_r.at[slot],
            device_id=(p, s), device_id_type=MESH,
        )

    def x_copy(d, slot):
        return pltpu.make_async_remote_copy(
            src_ref=block_out, dst_ref=x_state.at[slot],
            send_sem=x_s.at[d], recv_sem=x_r.at[slot],
            device_id=(g, row_mates[d]), device_id_type=MESH,
        )

    def xt_copy(d, slot):
        return pltpu.make_async_remote_copy(
            src_ref=tot_out, dst_ref=x_total.at[slot],
            send_sem=xt_s.at[d], recv_sem=xt_r.at[slot],
            device_id=(g, row_mates[d]), device_id_type=MESH,
        )

    def y_copy(d, slot):
        return pltpu.make_async_remote_copy(
            src_ref=row_out, dst_ref=y_state.at[slot],
            send_sem=y_s.at[d], recv_sem=y_r.at[slot],
            device_id=(g, column_mates[d]), device_id_type=MESH,
        )

    def yt_copy(d, slot):
        return pltpu.make_async_remote_copy(
            src_ref=rowtot_out, dst_ref=y_total.at[slot],
            send_sem=yt_s.at[d], recv_sem=yt_r.at[slot],
            device_id=(g, column_mates[d]), device_id_type=MESH,
        )

    greeters = len(same_core) + len(row_mates) + len(column_mates)
    far = [lax.rem(z + d, CHIPS) * 2 for d in (4, 3, 5)]
    near = [lax.rem(z + d, CHIPS) * 2 for d in (2, 6, 1, 7)]

    @pl.when(c == 0)
    def _():
        pl.semaphore_wait(barrier, greeters + CHIPS)
        for n in range(CHIPS):
            pl.semaphore_signal(gate, inc=1, device_id=(2 * n + 1, s), device_id_type=MESH)
        q_copy(far[0], g).start()
        q_copy(far[0] + 1, g).start()

    @pl.when(c == 1)
    def _():
        pl.semaphore_wait(barrier, greeters)
        q_copy(same_core[0], g).start()

    here = lax.broadcasted_iota(jnp.int32, (ROWS, ROWS), 0)
    there = lax.broadcasted_iota(jnp.int32, (ROWS, ROWS), 1)
    upto = (here <= there).astype(F32)
    decay_load.wait()
    chunk_levels = jnp.dot(
        decay_ref[...], upto, preferred_element_type=F32, precision=lax.Precision.HIGHEST
    )
    chunk_totals = jnp.broadcast_to(chunk_levels[:, ROWS - 1 : ROWS], (2 * GROUP, ROWS))
    level[...] = chunk_levels
    total[...] = chunk_totals
    for n in range(CHIPS):
        level_out[n, 0:4, :] = chunk_levels[4 * n : 4 * n + 4]
        level_out[n, 4:8, :] = chunk_levels[4 * n : 4 * n + 4]
    for h in range(2):
        block_total = chunk_totals[h : h + 1]
        for n in range(1, GROUP):
            block_total = block_total + chunk_totals[2 * n + h : 2 * n + h + 1]
        tot_out[4 * h : 4 * h + 4, :] = jnp.broadcast_to(block_total, (4, ROWS))
    level_in[g] = level_out[z]
    x_total[x] = tot_out[...]


    @pl.when(c == 0)
    def _():
        for p in same_core:
            level_copy(p, g).start()
        for n in range(CHIPS):
            level_copy(2 * n + 1, g).start()
        for d in range(X_SIZE - 1):
            xt_copy(d, x).start()
        for p in far[1:]:
            q_copy(p, g).start()
            q_copy(p + 1, g).start()

    @pl.when(c == 1)
    def _():
        for p in same_core:
            level_copy(p, g).start()
        for d in range(X_SIZE - 1):
            xt_copy(d, x).start()
        for p in same_core[1:]:
            q_copy(p, g).start()
        pl.semaphore_wait(gate, CHIPS)
        for n in range(CHIPS):
            level_copy(2 * n, g).start()
        for p in far:
            q_copy(p, g).start()

    for copy in loads:
        copy.wait()

    def owner(i):
        return lax.rem(z + order(2 * lax.rem(i, CHIPS))[0], CHIPS) * 2 + i // CHIPS

    def spread(row):
        wide = jnp.broadcast_to(row, (ROWS, ROWS))
        return wide, wide.T

    def head_cols(p, h):
        return pl.ds(pl.multiple_of(p * 2 * WIDTH + h * WIDTH, WIDTH), WIDTH)

    @pl.loop(0, GROUP)
    def _(i):
        p = owner(i)

        @pl.when(p != g)
        def _():
            level_copy(p, p).wait_recv()

        for h in range(2):
            _, down = spread(level_in[p, pl.ds(2 * c + h, 1), :])
            tail = jnp.exp(down[ROWS - 1 : ROWS, :] - down)
            scaled = (k_own[:, head_cols(p, h)].astype(F32) * tail).astype(BF16)
            state_own[p, h] = lax.dot_general(
                scaled, v_own[:, head_cols(p, h)], (((0,), (0,)), ((), ())),
                preferred_element_type=F32,
            )
        sib_copy(p).start()

    @pl.loop(0, GROUP)
    def _(i):
        p = owner(i)
        sib_copy(p).wait_recv()

        @pl.when(lax.rem(p, 2) == c)
        def _():
            for h in range(2):
                late = jnp.broadcast_to(level_in[p, 2 + h : 3 + h, ROWS - 1 : ROWS], (1, WIDTH))
                merged = (
                    jnp.exp(late * (1.0 - cf)) * state_own[p, h]
                    + jnp.exp(late * cf) * state_sib[p, h]
                )
                state_out[p // 2, h] = merged.astype(BF16)

            @pl.when(p != g)
            def _():
                state_copy(p // 2, z).start()

            @pl.when(p == g)
            def _():
                state_in[z] = state_out[z]

    @pl.when(c == 0)
    def _():
        for p in near:
            q_copy(p, g).start()
            q_copy(p + 1, g).start()
        q_copy(sibling, g).start()

    @pl.when(c == 1)
    def _():
        for p in near:
            q_copy(p, g).start()
        q_copy(sibling, g).start()

    causal = here >= there

    @pl.loop(0, GROUP)
    def _(i):
        p = peer(i)
        for h in range(2):
            wide, down = spread(level_in[p, pl.ds(2 * c + h, 1), :])
            q_head = q_own[:, head_cols(p, h)]
            scores = lax.dot_general(
                q_head, k_own[:, head_cols(p, h)], (((1,), (1,)), ((), ())),
                preferred_element_type=F32,
            )
            gap = jnp.where(causal, down - wide, 0.0)
            weights = jnp.where(causal, scores * jnp.exp(gap), 0.0).astype(BF16)
            part = jnp.dot(weights, v_own[:, head_cols(p, h)], preferred_element_type=F32)
            scaled = (q_head.astype(F32) * (jnp.exp(down) * cf)).astype(BF16)
            part = part + jnp.dot(
                scaled, state_sib[p, h].astype(BF16), preferred_element_type=F32
            )
            local_out[p, :, h * WIDTH : (h + 1) * WIDTH] = part.astype(BF16)

        @pl.when(i < GROUP - 1)
        def _():
            local_copy(p, g).start()

        @pl.when(i == GROUP - 1)
        def _():
            local_in[g] = local_out[g]

    @pl.loop(1, CHIPS)
    def _(d):
        chip = lax.rem(z + d, CHIPS)
        state_copy(chip, chip).wait_recv()

    def chip_share(n, h):
        return jnp.exp(total[4 * n + h : 4 * n + h + 1, :] + total[4 * n + 2 + h : 4 * n + 3 + h, :])

    for h in range(2):
        run = state_in[0, h].astype(F32)
        for n in range(1, CHIPS):
            run = chip_share(n, h) * run + state_in[n, h].astype(F32)
        block_out[h] = run.astype(BF16)
    for d in range(X_SIZE - 1):
        x_copy(d, x).start()
    x_state[x] = block_out[...]
    for d in range(1, X_SIZE):
        mate = lax.rem(x + d, X_SIZE)
        x_copy(d - 1, mate).wait_recv()
        xt_copy(d - 1, mate).wait_recv()

    for h in range(2):
        run = x_state[0, h].astype(F32)
        row_total = x_total[0, 4 * h : 4 * h + 1, :]
        for n in range(1, X_SIZE):
            here_total = x_total[n, 4 * h : 4 * h + 1, :]
            run = jnp.exp(here_total) * run + x_state[n, h].astype(F32)
            row_total = row_total + here_total
        row_out[h] = run.astype(BF16)
        rowtot_out[4 * h : 4 * h + 4, :] = jnp.broadcast_to(row_total, (4, ROWS))
    for d in range(Y_SIZE - 1):
        yt_copy(d, y).start()
        y_copy(d, y).start()
    y_state[y] = row_out[...]
    y_total[y] = rowtot_out[...]
    for d in range(1, Y_SIZE):
        mate = lax.rem(y + d, Y_SIZE)
        y_copy(d - 1, mate).wait_recv()
        yt_copy(d - 1, mate).wait_recv()

    for h in range(2):
        run = jnp.zeros((WIDTH, WIDTH), F32)
        for n in range(Y_SIZE - 1):
            used = (n < y).astype(F32)
            run = jnp.exp(y_total[n, 4 * h : 4 * h + 1, :] * used) * run + (
                y_state[n, h].astype(F32) * used
            )
        for n in range(X_SIZE - 1):
            used = (n < x).astype(F32)
            run = jnp.exp(x_total[n, 4 * h : 4 * h + 1, :] * used) * run + (
                x_state[n, h].astype(F32) * used
            )
        for n in range(CHIPS):
            prefix[n, h] = run.astype(BF16)
            run = chip_share(n, h) * run + state_in[n, h].astype(F32)

    @pl.loop(0, GROUP - 1)
    def _(i):
        p = source(i)
        q_copy(p, p).wait_recv()

    @pl.loop(0, GROUP)
    def _(p):
        chip, core = p // 2, lax.rem(p, 2)
        for h in range(2):
            row = level[pl.ds(2 * p + h, 1), :] + core.astype(F32) * total[pl.ds(4 * chip + h, 1), :]
            _, down = spread(row)
            scaled = (q_in[p, :, h * WIDTH : (h + 1) * WIDTH].astype(F32) * jnp.exp(down)).astype(BF16)
            carried[p, :, h * WIDTH : (h + 1) * WIDTH] = jnp.dot(
                scaled, prefix[chip, h], preferred_element_type=F32
            )

    def out_copy(p):
        return pltpu.make_async_copy(
            result.at[p], out_hbm.at[pl.ds(pl.multiple_of(p * ROWS, ROWS), ROWS), :], out_sem.at[p]
        )

    def finish(p):
        for h in range(2):
            part = slice(h * WIDTH, (h + 1) * WIDTH)
            mixture = carried[p, :, part] + local_in[p, :, part].astype(F32)
            mean_square = jnp.mean(mixture * mixture, axis=1, keepdims=True)
            normed = mixture * lax.rsqrt(mean_square + 1e-06) * gain_ref[:, part]
            result[p, :, part] = normed.astype(BF16)
        out_copy(p).start()

    finish(g)

    @pl.loop(0, GROUP)
    def _(p):
        sib_copy(p).wait_send()

    @pl.loop(0, GROUP - 1)
    def _(i):
        p = peer(i)
        level_copy(p, g).wait_send()
        q_copy(p, g).wait_send()

    @pl.loop(1, CHIPS)
    def _(d):
        state_copy(lax.rem(z + d, CHIPS), z).wait_send()

    for d in range(X_SIZE - 1):
        x_copy(d, x).wait_send()
        xt_copy(d, x).wait_send()
    for d in range(Y_SIZE - 1):
        y_copy(d, y).wait_send()
        yt_copy(d, y).wait_send()

    @pl.loop(0, GROUP - 1)
    def _(i):
        p = source(i)
        local_copy(peer(i), g).wait_send()
        local_copy(p, p).wait_recv()
        finish(p)

    @pl.loop(0, GROUP)
    def _(p):
        out_copy(p).wait()


def local(queries, keys, values, log_decay, gain):
    chunk_decay = log_decay.reshape(2, GROUP, ROWS).transpose(1, 0, 2).reshape(2 * GROUP, ROWS)
    any_space = pl.BlockSpec(memory_space=pl.ANY)
    dma = pltpu.SemaphoreType.DMA
    own = pltpu.VMEM((ROWS, GROUP * 2 * WIDTH), BF16)
    tile = pltpu.VMEM((8, ROWS), F32)
    return pl.pallas_call(
        kernel,
        out_shape=jax.ShapeDtypeStruct((GROUP * ROWS, 2 * WIDTH), BF16),
        in_specs=[any_space] * 5,
        out_specs=any_space,
        scratch_shapes=[
            pltpu.VMEM((2 * GROUP, ROWS), F32),
            pltpu.VMEM((1, 2 * WIDTH), F32),
            own, own, own,
            pltpu.VMEM((2 * GROUP, ROWS), F32),
            pltpu.VMEM((2 * GROUP, ROWS), F32),
            pltpu.VMEM((CHIPS, 8, ROWS), F32),
            pltpu.VMEM((GROUP, 8, ROWS), F32),
            pltpu.VMEM((GROUP, ROWS, 2 * WIDTH), BF16),
            pltpu.VMEM((GROUP, 2, WIDTH, WIDTH), F32),
            pltpu.VMEM((GROUP, 2, WIDTH, WIDTH), F32),
            pltpu.VMEM((CHIPS, 2, WIDTH, WIDTH), BF16),
            pltpu.VMEM((CHIPS, 2, WIDTH, WIDTH), BF16),
            pltpu.VMEM((GROUP, ROWS, 2 * WIDTH), BF16),
            pltpu.VMEM((GROUP, ROWS, 2 * WIDTH), BF16),
            pltpu.VMEM((2, WIDTH, WIDTH), BF16),
            pltpu.VMEM((X_SIZE, 2, WIDTH, WIDTH), BF16),
            pltpu.VMEM((X_SIZE, 8, ROWS), F32),
            pltpu.VMEM((2, WIDTH, WIDTH), BF16),
            pltpu.VMEM((Y_SIZE, 2, WIDTH, WIDTH), BF16),
            pltpu.VMEM((Y_SIZE, 8, ROWS), F32),
            tile, tile,
            pltpu.VMEM((CHIPS, 2, WIDTH, WIDTH), BF16),
            pltpu.VMEM((GROUP, ROWS, 2 * WIDTH), F32),
            pltpu.VMEM((GROUP, ROWS, 2 * WIDTH), BF16),
            dma((6,)),
            dma((GROUP,)), dma((GROUP,)),
            dma((GROUP,)), dma((GROUP,)),
            dma((GROUP,)), dma((GROUP,)),
            dma((CHIPS,)), dma((CHIPS,)),
            dma((GROUP,)), dma((GROUP,)),
            dma((X_SIZE,)), dma((X_SIZE,)), dma((X_SIZE,)), dma((X_SIZE,)),
            dma((Y_SIZE,)), dma((Y_SIZE,)), dma((Y_SIZE,)), dma((Y_SIZE,)),
            dma((GROUP,)),
            pltpu.SemaphoreType.REGULAR,
        ],
        compiler_params=pltpu.CompilerParams(
            collective_id=0, has_side_effects=True, vmem_limit_bytes=60 << 20
        ),
    )(queries, keys, values, chunk_decay, gain.reshape(1, 2 * WIDTH))


def solution(mesh):
    return jax.shard_map(
        local,
        mesh=mesh,
        in_specs=(
            P(("seq", "grp"), None), P(("seq", "grp"), None), P(("seq", "grp"), None),
            P("grp", "seq"), P("grp"),
        ),
        out_specs=P("seq", "grp"),
        check_vma=False,
    )
```

```python
import jax
import jax.numpy as jnp
from jax import lax
from jax.experimental import pallas as pl
from jax.experimental.pallas import tpu as pltpu
from jax.sharding import PartitionSpec as P

MESH = pl.DeviceIdType.MESH
F32 = jnp.float32
BF16 = jnp.bfloat16
CHIPS = 8
GROUP = 16
ROWS = 128
WIDTH = 128
X_SIZE = 4
Y_SIZE = 8
KEPT, SENT = 1, 0


def order(i):
    m = i // 2
    odd = m % 2
    return 4 + (1 - 2 * odd) * ((m + 1) // 2), 1 - i % 2


def kernel(
    q_hbm, k_hbm, v_hbm, decay_hbm, gain_hbm, out_hbm,
    decay_ref, gain_ref,
    q_own, k_own, v_own, level, total, level_out, level_in,
    q_in, state_own, state_sib, state_out, state_in, local_out, local_in, local_kept,
    block_out, x_state, x_total, row_out, y_state, y_total, tot_out, rowtot_out,
    prefix, entering, carried, result, result_kept,
    load_sem, level_s, level_r, q_s, q_r, sib_s, sib_r, state_s, state_r, local_s, local_r,
    x_s, x_r, xt_s, xt_r, y_s, y_r, yt_s, yt_r, enter_s, enter_r, pass_s, done_s, done_r,
    out_sem, hand_s, gate, sib_gate,
):
    g = lax.axis_index("grp")
    s = lax.axis_index("seq")
    z, c = g // 2, lax.rem(g, 2)
    y, x = s // X_SIZE, lax.rem(s, X_SIZE)
    cf = c.astype(F32)
    sibling = g + 1 - 2 * c

    def peer(i):
        dz, dc = order(i)
        return lax.rem(z + dz, CHIPS) * 2 + lax.rem(c + dc, 2)

    def source(i):
        dz, dc = order(i)
        return lax.rem(z + 2 * CHIPS - dz, CHIPS) * 2 + lax.rem(c + dc, 2)

    def cols(p, h):
        return pl.ds(pl.multiple_of(p * 2 * WIDTH + h * WIDTH, WIDTH), WIDTH)

    def rows(p):
        return pl.ds(pl.multiple_of(p * ROWS, ROWS), ROWS)

    def side(h):
        return pl.ds(h * WIDTH, WIDTH)

    barrier = pltpu.get_barrier_semaphore()
    row_mates = [y * X_SIZE + lax.rem(x + d, X_SIZE) for d in range(1, X_SIZE)]
    column_mates = [lax.rem(y + d, Y_SIZE) * X_SIZE + x for d in range(1, Y_SIZE)]
    same_core = [lax.rem(z + d, CHIPS) * 2 + c for d in (4, 3, 5, 2, 6, 1, 7)]
    zeros = [lax.rem(z + d, CHIPS) * 2 for d in (4, 3, 5, 2, 6, 1, 7)]
    for p in same_core:
        pl.semaphore_signal(barrier, inc=1, device_id=(p, s), device_id_type=MESH)

    @pl.when(c == 1)
    def _():
        for n in range(CHIPS):
            pl.semaphore_signal(barrier, inc=1, device_id=(2 * n, s), device_id_type=MESH)

    for m in row_mates + column_mates:
        pl.semaphore_signal(barrier, inc=1, device_id=(g, m), device_id_type=MESH)
    greeters = len(same_core) + len(row_mates) + len(column_mates)

    decay_load = pltpu.make_async_copy(decay_hbm, decay_ref, load_sem.at[0])
    gain_load = pltpu.make_async_copy(gain_hbm, gain_ref, load_sem.at[1])
    loads = [
        pltpu.make_async_copy(k_hbm, k_own, load_sem.at[2]),
        pltpu.make_async_copy(v_hbm, v_own, load_sem.at[3]),
        pltpu.make_async_copy(q_hbm, q_own, load_sem.at[4]),
        pltpu.make_async_copy(q_hbm.at[:, cols(g, SENT)], q_in.at[g], load_sem.at[5]),
    ]
    for copy in [decay_load, gain_load] + loads:
        copy.start()

    def level_copy(p, slot):
        return pltpu.make_async_remote_copy(
            src_ref=level_out.at[p // 2], dst_ref=level_in.at[slot],
            send_sem=level_s.at[p], recv_sem=level_r.at[slot],
            device_id=(p, s), device_id_type=MESH,
        )

    def hand_copy(p):
        return pltpu.make_async_remote_copy(
            src_ref=level_in.at[p], dst_ref=level_in.at[p],
            send_sem=hand_s.at[p], recv_sem=level_r.at[p],
            device_id=(sibling, s), device_id_type=MESH,
        )

    def q_copy(p, slot):
        return pltpu.make_async_remote_copy(
            src_ref=q_hbm.at[:, cols(p, SENT)], dst_ref=q_in.at[slot],
            send_sem=q_s.at[p], recv_sem=q_r.at[slot],
            device_id=(p, s), device_id_type=MESH,
        )

    def sib_copy(p):
        return pltpu.make_async_remote_copy(
            src_ref=state_own.at[p], dst_ref=state_sib.at[p],
            send_sem=sib_s.at[p], recv_sem=sib_r.at[p],
            device_id=(sibling, s), device_id_type=MESH,
        )

    def state_copy(h, chip, slot):
        return pltpu.make_async_remote_copy(
            src_ref=state_out.at[h, chip], dst_ref=state_in.at[h, slot],
            send_sem=state_s.at[h, chip], recv_sem=state_r.at[h, slot],
            device_id=(chip * 2 + c, s), device_id_type=MESH,
        )

    def local_copy(p, slot):
        return pltpu.make_async_remote_copy(
            src_ref=local_out.at[p], dst_ref=local_in.at[slot],
            send_sem=local_s.at[p], recv_sem=local_r.at[slot],
            device_id=(p, s), device_id_type=MESH,
        )

    def x_copy(h, d, slot):
        return pltpu.make_async_remote_copy(
            src_ref=block_out.at[h], dst_ref=x_state.at[h, slot],
            send_sem=x_s.at[h, d], recv_sem=x_r.at[h, slot],
            device_id=(g, row_mates[d]), device_id_type=MESH,
        )

    def xt_copy(d, slot):
        return pltpu.make_async_remote_copy(
            src_ref=tot_out, dst_ref=x_total.at[slot],
            send_sem=xt_s.at[d], recv_sem=xt_r.at[slot],
            device_id=(g, row_mates[d]), device_id_type=MESH,
        )

    def y_copy(h, d, slot):
        return pltpu.make_async_remote_copy(
            src_ref=row_out.at[h], dst_ref=y_state.at[h, slot],
            send_sem=y_s.at[h, d], recv_sem=y_r.at[h, slot],
            device_id=(g, column_mates[d]), device_id_type=MESH,
        )

    def yt_copy(d, slot):
        return pltpu.make_async_remote_copy(
            src_ref=rowtot_out, dst_ref=y_total.at[slot],
            send_sem=yt_s.at[d], recv_sem=yt_r.at[slot],
            device_id=(g, column_mates[d]), device_id_type=MESH,
        )

    def enter_copy(chip, slot):
        return pltpu.make_async_remote_copy(
            src_ref=prefix.at[KEPT, chip], dst_ref=entering.at[slot],
            send_sem=enter_s.at[chip], recv_sem=enter_r.at[slot],
            device_id=(chip * 2 + c, s), device_id_type=MESH,
        )

    def pass_copy(p):
        return pltpu.make_async_remote_copy(
            src_ref=entering.at[p], dst_ref=entering.at[p],
            send_sem=pass_s.at[p], recv_sem=enter_r.at[p],
            device_id=(sibling, s), device_id_type=MESH,
        )

    def done_copy(p, slot):
        return pltpu.make_async_remote_copy(
            src_ref=result_kept.at[p], dst_ref=out_hbm.at[rows(slot), side(KEPT)],
            send_sem=done_s.at[p], recv_sem=done_r.at[slot],
            device_id=(p, s), device_id_type=MESH,
        )

    @pl.when(c == 0)
    def _():
        pl.semaphore_wait(barrier, greeters + CHIPS)
        pl.semaphore_signal(sib_gate, inc=1, device_id=(sibling, s), device_id_type=MESH)
        for n in range(CHIPS):
            pl.semaphore_signal(gate, inc=1, device_id=(2 * n + 1, s), device_id_type=MESH)
        q_copy(zeros[0], g).start()
        q_copy(zeros[0] + 1, g).start()

    @pl.when(c == 1)
    def _():
        pl.semaphore_wait(barrier, greeters)
        q_copy(same_core[0], g).start()

    here = lax.broadcasted_iota(jnp.int32, (ROWS, ROWS), 0)
    there = lax.broadcasted_iota(jnp.int32, (ROWS, ROWS), 1)
    upto = (here <= there).astype(F32)
    decay_load.wait()
    gain_load.wait()
    chunk_levels = jnp.dot(
        decay_ref[...], upto, preferred_element_type=F32, precision=lax.Precision.HIGHEST
    )
    chunk_totals = jnp.broadcast_to(chunk_levels[:, ROWS - 1 : ROWS], (2 * GROUP, ROWS))
    level[...] = chunk_levels
    total[...] = chunk_totals
    gain_kept = jnp.broadcast_to(gain_ref[:, KEPT * WIDTH : (KEPT + 1) * WIDTH], (4, WIDTH))
    for n in range(CHIPS):
        level_out[n, 0:4, :] = chunk_levels[4 * n : 4 * n + 4]
        level_out[n, 4:8, :] = gain_kept
    for h in range(2):
        block_total = chunk_totals[h : h + 1]
        for n in range(1, GROUP):
            block_total = block_total + chunk_totals[2 * n + h : 2 * n + h + 1]
        tot_out[4 * h : 4 * h + 4, :] = jnp.broadcast_to(block_total, (4, ROWS))
    level_in[g] = level_out[z]
    x_total[x] = tot_out[...]

    @pl.when(c == 0)
    def _():
        for p in same_core:
            level_copy(p, g).start()
        for n in range(CHIPS):
            level_copy(2 * n + 1, g).start()
        for d in range(X_SIZE - 1):
            xt_copy(d, x).start()
        for p in zeros[1:]:
            q_copy(p, g).start()
            q_copy(p + 1, g).start()
        q_copy(sibling, g).start()

    @pl.when(c == 1)
    def _():
        for p in same_core:
            level_copy(p, g).start()
        for d in range(X_SIZE - 1):
            xt_copy(d, x).start()
        for p in same_core[1:3]:
            q_copy(p, g).start()
        for p in same_core:
            level_copy(p, p).wait_recv()
        pl.semaphore_wait(sib_gate, 1)
        for n in range(CHIPS):
            hand_copy(2 * n + 1).start()
        for p in same_core[3:]:
            q_copy(p, g).start()
        pl.semaphore_wait(gate, CHIPS)
        for p in zeros:
            q_copy(p, g).start()
        q_copy(sibling, g).start()

    for copy in loads:
        copy.wait()

    def owner(i):
        return lax.rem(z + order(2 * lax.rem(i, CHIPS))[0], CHIPS) * 2 + 1 - i // CHIPS

    def chip_at(i):
        return lax.rem(z + order(2 * i)[0], CHIPS)

    def spread(row):
        wide = jnp.broadcast_to(row, (ROWS, ROWS))
        return wide, wide.T

    @pl.loop(0, GROUP)
    def _(i):
        p = owner(i)

        @pl.when(jnp.logical_or(
            jnp.logical_and(c == 0, p != g), jnp.logical_and(c == 1, lax.rem(p, 2) == 0)
        ))
        def _():
            level_copy(p, p).wait_recv()

        for h in range(2):
            _, down = spread(level_in[p, pl.ds(2 * c + h, 1), :])
            tail = jnp.exp(down[ROWS - 1 : ROWS, :] - down)
            scaled = (k_own[:, cols(p, h)].astype(F32) * tail).astype(BF16)
            state_own[p, h] = lax.dot_general(
                scaled, v_own[:, cols(p, h)], (((0,), (0,)), ((), ())),
                preferred_element_type=F32,
            )
        sib_copy(p).start()

    @pl.loop(0, GROUP)
    def _(i):
        sib_copy(owner(i)).wait_recv()

    for h in (KEPT, SENT):
        @pl.loop(0, CHIPS)
        def _(i):
            chip = chip_at(i)
            p = chip * 2 + c
            late = jnp.broadcast_to(level_in[p, 2 + h : 3 + h, ROWS - 1 : ROWS], (1, WIDTH))
            merged = (
                jnp.exp(late * (1.0 - cf)) * state_own[p, h]
                + jnp.exp(late * cf) * state_sib[p, h]
            )
            state_out[h, chip] = merged.astype(BF16)

            @pl.when(i < CHIPS - 1)
            def _():
                state_copy(h, chip, z).start()

            @pl.when(i == CHIPS - 1)
            def _():
                state_in[h, z] = state_out[h, z]

    causal = here >= there

    def inside(p, h):
        wide, down = spread(level_in[p, pl.ds(2 * c + h, 1), :])
        q_head = q_own[:, cols(p, h)]
        scores = lax.dot_general(
            q_head, k_own[:, cols(p, h)], (((1,), (1,)), ((), ())),
            preferred_element_type=F32,
        )
        gap = jnp.where(causal, down - wide, 0.0)
        weights = jnp.where(causal, scores * jnp.exp(gap), 0.0).astype(BF16)
        part = jnp.dot(weights, v_own[:, cols(p, h)], preferred_element_type=F32)
        scaled = (q_head.astype(F32) * (jnp.exp(down) * cf)).astype(BF16)
        return part + jnp.dot(
            scaled, state_sib[p, h].astype(BF16), preferred_element_type=F32
        )

    @pl.loop(0, GROUP)
    def _(i):
        p = peer(i)
        local_out[p] = inside(p, SENT).astype(BF16)

        @pl.when(i < GROUP - 1)
        def _():
            local_copy(p, g).start()

        @pl.when(i == GROUP - 1)
        def _():
            local_in[g] = local_out[g]

    @pl.loop(0, GROUP)
    def _(p):
        local_kept[p] = inside(p, KEPT)

    def chip_share(n, h):
        return jnp.exp(total[4 * n + h : 4 * n + h + 1, :] + total[4 * n + 2 + h : 4 * n + 3 + h, :])

    def send_block(h):
        @pl.loop(1, CHIPS)
        def _(d):
            chip = lax.rem(z + d, CHIPS)
            state_copy(h, chip, chip).wait_recv()

        run = state_in[h, 0].astype(F32)
        for n in range(1, CHIPS):
            run = chip_share(n, h) * run + state_in[h, n].astype(F32)
        block_out[h] = run.astype(BF16)
        for d in range(X_SIZE - 1):
            x_copy(h, d, x).start()
        x_state[h, x] = block_out[h]

    def send_row(h):
        for d in range(1, X_SIZE):
            x_copy(h, d - 1, lax.rem(x + d, X_SIZE)).wait_recv()
        run = x_state[h, 0].astype(F32)
        for n in range(1, X_SIZE):
            run = jnp.exp(x_total[n, 4 * h : 4 * h + 1, :]) * run + x_state[h, n].astype(F32)
        row_out[h] = run.astype(BF16)
        for d in range(Y_SIZE - 1):
            y_copy(h, d, y).start()
        y_state[h, y] = row_out[h]

    def enter(h):
        for d in range(Y_SIZE - 1):
            y_copy(h, d, lax.rem(y + d + 1, Y_SIZE)).wait_recv()
        run = jnp.zeros((WIDTH, WIDTH), F32)
        for n in range(Y_SIZE - 1):
            used = (n < y).astype(F32)
            run = jnp.exp(y_total[n, 4 * h : 4 * h + 1, :] * used) * run + (
                y_state[h, n].astype(F32) * used
            )
        for n in range(X_SIZE - 1):
            used = (n < x).astype(F32)
            run = jnp.exp(x_total[n, 4 * h : 4 * h + 1, :] * used) * run + (
                x_state[h, n].astype(F32) * used
            )
        for n in range(CHIPS):
            prefix[h, n] = run.astype(BF16)
            run = chip_share(n, h) * run + state_in[h, n].astype(F32)

    for d in range(1, X_SIZE):
        xt_copy(d - 1, lax.rem(x + d, X_SIZE)).wait_recv()
    for h in range(2):
        row_total = x_total[0, 4 * h : 4 * h + 1, :]
        for n in range(1, X_SIZE):
            row_total = row_total + x_total[n, 4 * h : 4 * h + 1, :]
        rowtot_out[4 * h : 4 * h + 4, :] = jnp.broadcast_to(row_total, (4, ROWS))
    for d in range(Y_SIZE - 1):
        yt_copy(d, y).start()
    y_total[y] = rowtot_out[...]

    send_block(KEPT)
    for d in range(Y_SIZE - 1):
        yt_copy(d, lax.rem(y + d + 1, Y_SIZE)).wait_recv()
    send_row(KEPT)
    send_block(SENT)
    enter(KEPT)

    @pl.loop(0, CHIPS - 1)
    def _(i):
        enter_copy(chip_at(i), g).start()

    entering[g] = prefix[KEPT, z]
    send_row(SENT)

    def finish_kept(p):
        row = level_in[p, pl.ds(2 * c + KEPT, 1), :] + cf * jnp.broadcast_to(
            level_in[p, KEPT : KEPT + 1, ROWS - 1 : ROWS], (1, ROWS)
        )
        _, down = spread(row)
        scaled = (q_own[:, cols(p, KEPT)].astype(F32) * jnp.exp(down)).astype(BF16)
        mixture = local_kept[p] + jnp.dot(scaled, entering[p], preferred_element_type=F32)
        mean_square = jnp.mean(mixture * mixture, axis=1, keepdims=True)
        normed = mixture * lax.rsqrt(mean_square + 1e-06) * level_in[p, 4:5, :]
        result_kept[p] = normed.astype(BF16)

    def own_done():
        return pltpu.make_async_copy(
            result_kept.at[g], out_hbm.at[rows(g), side(KEPT)], done_s.at[g]
        )

    pass_copy(g).start()

    @pl.loop(0, CHIPS - 1)
    def _(i):
        p = lax.rem(z + 2 * CHIPS - order(2 * i)[0], CHIPS) * 2 + c
        enter_copy(0, p).wait_recv()
        pass_copy(p).start()
        finish_kept(p)
        done_copy(p, g).start()

    @pl.loop(0, CHIPS)
    def _(i):
        p = lax.rem(z + 2 * CHIPS - order(2 * i)[0], CHIPS) * 2 + 1 - c
        pass_copy(p).wait_recv()
        finish_kept(p)
        done_copy(p, g).start()

    finish_kept(g)
    own_done().start()

    enter(SENT)

    @pl.loop(0, GROUP - 1)
    def _(i):
        p = source(i)
        q_copy(p, p).wait_recv()

    @pl.loop(0, GROUP)
    def _(p):
        chip, core = p // 2, lax.rem(p, 2)
        row = level[pl.ds(2 * p + SENT, 1), :] + (
            core.astype(F32) * total[pl.ds(4 * chip + SENT, 1), :]
        )
        _, down = spread(row)
        scaled = (q_in[p].astype(F32) * jnp.exp(down)).astype(BF16)
        carried[p] = jnp.dot(scaled, prefix[SENT, chip], preferred_element_type=F32)

    def out_copy(p):
        return pltpu.make_async_copy(
            result.at[p], out_hbm.at[rows(p), side(SENT)], out_sem.at[p]
        )

    def finish_sent(p):
        mixture = carried[p] + local_in[p].astype(F32)
        mean_square = jnp.mean(mixture * mixture, axis=1, keepdims=True)
        normed = mixture * lax.rsqrt(mean_square + 1e-06) * gain_ref[:, 0:WIDTH]
        result[p] = normed.astype(BF16)
        out_copy(p).start()

    finish_sent(g)

    @pl.loop(0, GROUP - 1)
    def _(i):
        p = source(i)
        local_copy(p, p).wait_recv()
        finish_sent(p)

    @pl.loop(0, GROUP)
    def _(p):
        sib_copy(p).wait_send()

    @pl.loop(0, GROUP - 1)
    def _(i):
        p = peer(i)

        @pl.when(jnp.logical_or(c == 0, lax.rem(p, 2) == 1))
        def _():
            level_copy(p, g).wait_send()

        q_copy(p, g).wait_send()
        local_copy(p, g).wait_send()

    @pl.when(c == 1)
    def _():
        for n in range(CHIPS):
            hand_copy(2 * n + 1).wait_send()

    for h in range(2):
        @pl.loop(0, CHIPS - 1)
        def _(i):
            state_copy(h, chip_at(i), z).wait_send()

        for d in range(X_SIZE - 1):
            x_copy(h, d, x).wait_send()
        for d in range(Y_SIZE - 1):
            y_copy(h, d, y).wait_send()

    @pl.loop(0, CHIPS - 1)
    def _(i):
        enter_copy(chip_at(i), g).wait_send()

    @pl.loop(0, CHIPS)
    def _(n):
        pass_copy(2 * n + c).wait_send()

    for d in range(X_SIZE - 1):
        xt_copy(d, x).wait_send()
    for d in range(Y_SIZE - 1):
        yt_copy(d, y).wait_send()
    own_done().wait()

    @pl.loop(0, GROUP)
    def _(p):
        out_copy(p).wait()

    @pl.loop(0, GROUP - 1)
    def _(i):
        p = source(i)
        done_copy(peer(i), g).wait_send()
        done_copy(p, p).wait_recv()


def local(queries, keys, values, log_decay, gain):
    chunk_decay = log_decay.reshape(2, GROUP, ROWS).transpose(1, 0, 2).reshape(2 * GROUP, ROWS)
    any_space = pl.BlockSpec(memory_space=pl.ANY)
    dma = pltpu.SemaphoreType.DMA
    own = pltpu.VMEM((ROWS, GROUP * 2 * WIDTH), BF16)
    tile = pltpu.VMEM((8, ROWS), F32)

    def parts(*lead):
        return pltpu.VMEM((*lead, ROWS, WIDTH), BF16)

    def wide_parts(*lead):
        return pltpu.VMEM((*lead, ROWS, WIDTH), F32)

    return pl.pallas_call(
        kernel,
        out_shape=jax.ShapeDtypeStruct((GROUP * ROWS, 2 * WIDTH), BF16),
        in_specs=[any_space] * 5,
        out_specs=any_space,
        scratch_shapes=[
            pltpu.VMEM((2 * GROUP, ROWS), F32),
            pltpu.VMEM((1, 2 * WIDTH), F32),
            own, own, own,
            pltpu.VMEM((2 * GROUP, ROWS), F32),
            pltpu.VMEM((2 * GROUP, ROWS), F32),
            pltpu.VMEM((CHIPS, 8, ROWS), F32),
            pltpu.VMEM((GROUP, 8, ROWS), F32),
            parts(GROUP),
            wide_parts(GROUP, 2), wide_parts(GROUP, 2),
            parts(2, CHIPS), parts(2, CHIPS),
            parts(GROUP), parts(GROUP), wide_parts(GROUP),
            parts(2), parts(2, X_SIZE),
            pltpu.VMEM((X_SIZE, 8, ROWS), F32),
            parts(2), parts(2, Y_SIZE),
            pltpu.VMEM((Y_SIZE, 8, ROWS), F32),
            tile, tile,
            parts(2, CHIPS), parts(GROUP), wide_parts(GROUP), parts(GROUP), parts(GROUP),
            dma((6,)),
            dma((GROUP,)), dma((GROUP,)),
            dma((GROUP,)), dma((GROUP,)),
            dma((GROUP,)), dma((GROUP,)),
            dma((2, CHIPS)), dma((2, CHIPS)),
            dma((GROUP,)), dma((GROUP,)),
            dma((2, X_SIZE)), dma((2, X_SIZE)), dma((X_SIZE,)), dma((X_SIZE,)),
            dma((2, Y_SIZE)), dma((2, Y_SIZE)), dma((Y_SIZE,)), dma((Y_SIZE,)),
            dma((CHIPS,)), dma((GROUP,)), dma((GROUP,)), dma((GROUP,)), dma((GROUP,)),
            dma((GROUP,)), dma((GROUP,)),
            pltpu.SemaphoreType.REGULAR, pltpu.SemaphoreType.REGULAR,
        ],
        compiler_params=pltpu.CompilerParams(
            collective_id=0, has_side_effects=True, vmem_limit_bytes=60 << 20
        ),
    )(queries, keys, values, chunk_decay, gain.reshape(1, 2 * WIDTH))


def solution(mesh):
    return jax.shard_map(
        local,
        mesh=mesh,
        in_specs=(
            P(("seq", "grp"), None), P(("seq", "grp"), None), P(("seq", "grp"), None),
            P("grp", "seq"), P("grp"),
        ),
        out_specs=P("seq", "grp"),
        check_vma=False,
    )
```

```python
import jax
import jax.numpy as jnp
from jax import lax
from jax.experimental import pallas as pl
from jax.experimental.pallas import tpu as pltpu
from jax.sharding import PartitionSpec as P

MESH = pl.DeviceIdType.MESH
F32 = jnp.float32
BF16 = jnp.bfloat16
CHIPS = 8
GROUP = 16
ROWS = 128
WIDTH = 128
X_SIZE = 4
SHARE = WIDTH // X_SIZE
Y_SIZE = 8
KEPT, SENT = 1, 0


def order(i):
    m = i // 2
    odd = m % 2
    return 4 + (1 - 2 * odd) * ((m + 1) // 2), 1 - i % 2


def kernel(
    q_hbm, k_hbm, v_hbm, decay_hbm, gain_hbm, out_hbm,
    decay_ref, gain_ref,
    q_own, k_own, v_own, level, total, level_out, level_in,
    q_in, state_own, state_sib, state_out, state_in, local_out, local_in, local_kept,
    block_out, x_state, x_total, row_out, y_state, y_total, tot_out, rowtot_out,
    cross_out, cross_in,
    prefix, entering, carried, result, result_kept,
    load_sem, level_s, level_r, q_s, q_r, sib_s, sib_r, state_s, state_r, local_s, local_r,
    x_s, x_r, xt_s, xt_r, y_s, y_r, yt_s, yt_r, cross_s, cross_r, enter_s, enter_r, pass_s, done_s, done_r,
    out_sem, hand_s, gate, sib_gate,
):
    g = lax.axis_index("grp")
    s = lax.axis_index("seq")
    z, c = g // 2, lax.rem(g, 2)
    y, x = s // X_SIZE, lax.rem(s, X_SIZE)
    cf = c.astype(F32)
    sibling = g + 1 - 2 * c

    def peer(i):
        dz, dc = order(i)
        return lax.rem(z + dz, CHIPS) * 2 + lax.rem(c + dc, 2)

    def source(i):
        dz, dc = order(i)
        return lax.rem(z + 2 * CHIPS - dz, CHIPS) * 2 + lax.rem(c + dc, 2)

    def cols(p, h):
        return pl.ds(pl.multiple_of(p * 2 * WIDTH + h * WIDTH, WIDTH), WIDTH)

    def rows(p):
        return pl.ds(pl.multiple_of(p * ROWS, ROWS), ROWS)

    def side(h):
        return pl.ds(h * WIDTH, WIDTH)

    barrier = pltpu.get_barrier_semaphore()
    row_mates = [y * X_SIZE + lax.rem(x + d, X_SIZE) for d in range(1, X_SIZE)]
    column_mates = [lax.rem(y + d, Y_SIZE) * X_SIZE + x for d in range(1, Y_SIZE)]
    same_core = [lax.rem(z + d, CHIPS) * 2 + c for d in (4, 3, 5, 2, 6, 1, 7)]
    zeros = [lax.rem(z + d, CHIPS) * 2 for d in (4, 3, 5, 2, 6, 1, 7)]
    for p in same_core:
        pl.semaphore_signal(barrier, inc=1, device_id=(p, s), device_id_type=MESH)

    @pl.when(c == 1)
    def _():
        for n in range(CHIPS):
            pl.semaphore_signal(barrier, inc=1, device_id=(2 * n, s), device_id_type=MESH)

    for m in row_mates + column_mates:
        pl.semaphore_signal(barrier, inc=1, device_id=(g, m), device_id_type=MESH)
    greeters = len(same_core) + len(row_mates) + len(column_mates)

    decay_load = pltpu.make_async_copy(decay_hbm, decay_ref, load_sem.at[0])
    gain_load = pltpu.make_async_copy(gain_hbm, gain_ref, load_sem.at[1])
    loads = [
        pltpu.make_async_copy(k_hbm, k_own, load_sem.at[2]),
        pltpu.make_async_copy(v_hbm, v_own, load_sem.at[3]),
        pltpu.make_async_copy(q_hbm, q_own, load_sem.at[4]),
        pltpu.make_async_copy(q_hbm.at[:, cols(g, SENT)], q_in.at[g], load_sem.at[5]),
    ]
    for copy in [decay_load, gain_load] + loads:
        copy.start()

    def level_copy(p, slot):
        return pltpu.make_async_remote_copy(
            src_ref=level_out.at[p // 2], dst_ref=level_in.at[slot],
            send_sem=level_s.at[p], recv_sem=level_r.at[slot],
            device_id=(p, s), device_id_type=MESH,
        )

    def hand_copy(p):
        return pltpu.make_async_remote_copy(
            src_ref=level_in.at[p], dst_ref=level_in.at[p],
            send_sem=hand_s.at[p], recv_sem=level_r.at[p],
            device_id=(sibling, s), device_id_type=MESH,
        )

    def q_copy(p, slot):
        return pltpu.make_async_remote_copy(
            src_ref=q_hbm.at[:, cols(p, SENT)], dst_ref=q_in.at[slot],
            send_sem=q_s.at[p], recv_sem=q_r.at[slot],
            device_id=(p, s), device_id_type=MESH,
        )

    def sib_copy(p):
        return pltpu.make_async_remote_copy(
            src_ref=state_own.at[p], dst_ref=state_sib.at[p],
            send_sem=sib_s.at[p], recv_sem=sib_r.at[p],
            device_id=(sibling, s), device_id_type=MESH,
        )

    def state_copy(h, chip, slot):
        return pltpu.make_async_remote_copy(
            src_ref=state_out.at[h, chip], dst_ref=state_in.at[h, slot],
            send_sem=state_s.at[h, chip], recv_sem=state_r.at[h, slot],
            device_id=(chip * 2 + c, s), device_id_type=MESH,
        )

    def local_copy(p, slot):
        return pltpu.make_async_remote_copy(
            src_ref=local_out.at[p], dst_ref=local_in.at[slot],
            send_sem=local_s.at[p], recv_sem=local_r.at[slot],
            device_id=(p, s), device_id_type=MESH,
        )

    def share(n):
        return pl.ds(pl.multiple_of(n * SHARE, SHARE), SHARE)

    def cross_copy(h, d, slot):
        return pltpu.make_async_remote_copy(
            src_ref=cross_out.at[h, lax.rem(x + d + 1, X_SIZE)],
            dst_ref=cross_in.at[h, slot],
            send_sem=cross_s.at[h, d], recv_sem=cross_r.at[h, slot],
            device_id=(g, row_mates[d]), device_id_type=MESH,
        )

    def x_copy(h, d, slot):
        return pltpu.make_async_remote_copy(
            src_ref=block_out.at[h, share(lax.rem(x + d + 1, X_SIZE)), :],
            dst_ref=x_state.at[h, slot],
            send_sem=x_s.at[h, d], recv_sem=x_r.at[h, slot],
            device_id=(g, row_mates[d]), device_id_type=MESH,
        )

    def xt_copy(d, slot):
        return pltpu.make_async_remote_copy(
            src_ref=tot_out, dst_ref=x_total.at[slot],
            send_sem=xt_s.at[d], recv_sem=xt_r.at[slot],
            device_id=(g, row_mates[d]), device_id_type=MESH,
        )

    def y_copy(h, d, slot):
        return pltpu.make_async_remote_copy(
            src_ref=row_out.at[h], dst_ref=y_state.at[h, slot],
            send_sem=y_s.at[h, d], recv_sem=y_r.at[h, slot],
            device_id=(g, column_mates[d]), device_id_type=MESH,
        )

    def yt_copy(d, slot):
        return pltpu.make_async_remote_copy(
            src_ref=rowtot_out, dst_ref=y_total.at[slot],
            send_sem=yt_s.at[d], recv_sem=yt_r.at[slot],
            device_id=(g, column_mates[d]), device_id_type=MESH,
        )

    def enter_copy(chip, slot):
        return pltpu.make_async_remote_copy(
            src_ref=prefix.at[KEPT, chip], dst_ref=entering.at[slot],
            send_sem=enter_s.at[chip], recv_sem=enter_r.at[slot],
            device_id=(chip * 2 + c, s), device_id_type=MESH,
        )

    def pass_copy(p):
        return pltpu.make_async_remote_copy(
            src_ref=entering.at[p], dst_ref=entering.at[p],
            send_sem=pass_s.at[p], recv_sem=enter_r.at[p],
            device_id=(sibling, s), device_id_type=MESH,
        )

    def done_copy(p, slot):
        return pltpu.make_async_remote_copy(
            src_ref=result_kept.at[p], dst_ref=out_hbm.at[rows(slot), side(KEPT)],
            send_sem=done_s.at[p], recv_sem=done_r.at[slot],
            device_id=(p, s), device_id_type=MESH,
        )

    @pl.when(c == 0)
    def _():
        pl.semaphore_wait(barrier, greeters + CHIPS)
        pl.semaphore_signal(sib_gate, inc=1, device_id=(sibling, s), device_id_type=MESH)
        for n in range(CHIPS):
            pl.semaphore_signal(gate, inc=1, device_id=(2 * n + 1, s), device_id_type=MESH)
        q_copy(zeros[0], g).start()
        q_copy(zeros[0] + 1, g).start()

    @pl.when(c == 1)
    def _():
        pl.semaphore_wait(barrier, greeters)
        q_copy(same_core[0], g).start()

    here = lax.broadcasted_iota(jnp.int32, (ROWS, ROWS), 0)
    there = lax.broadcasted_iota(jnp.int32, (ROWS, ROWS), 1)
    upto = (here <= there).astype(F32)
    decay_load.wait()
    gain_load.wait()
    chunk_levels = jnp.dot(
        decay_ref[...], upto, preferred_element_type=F32, precision=lax.Precision.HIGHEST
    )
    chunk_totals = jnp.broadcast_to(chunk_levels[:, ROWS - 1 : ROWS], (2 * GROUP, ROWS))
    level[...] = chunk_levels
    total[...] = chunk_totals
    gain_kept = jnp.broadcast_to(gain_ref[:, KEPT * WIDTH : (KEPT + 1) * WIDTH], (4, WIDTH))
    for n in range(CHIPS):
        level_out[n, 0:4, :] = chunk_levels[4 * n : 4 * n + 4]
        level_out[n, 4:8, :] = gain_kept
    for h in range(2):
        block_total = chunk_totals[h : h + 1]
        for n in range(1, GROUP):
            block_total = block_total + chunk_totals[2 * n + h : 2 * n + h + 1]
        tot_out[4 * h : 4 * h + 4, :] = jnp.broadcast_to(block_total, (4, ROWS))
    level_in[g] = level_out[z]
    x_total[x] = tot_out[...]

    @pl.when(c == 0)
    def _():
        for p in same_core:
            level_copy(p, g).start()
        for n in range(CHIPS):
            level_copy(2 * n + 1, g).start()
        for d in range(X_SIZE - 1):
            xt_copy(d, x).start()
        for p in zeros[1:]:
            q_copy(p, g).start()
            q_copy(p + 1, g).start()
        q_copy(sibling, g).start()

    @pl.when(c == 1)
    def _():
        for p in same_core:
            level_copy(p, g).start()
        for d in range(X_SIZE - 1):
            xt_copy(d, x).start()
        for p in same_core[1:3]:
            q_copy(p, g).start()
        for p in same_core:
            level_copy(p, p).wait_recv()
        pl.semaphore_wait(sib_gate, 1)
        for n in range(CHIPS):
            hand_copy(2 * n + 1).start()
        for p in same_core[3:]:
            q_copy(p, g).start()
        pl.semaphore_wait(gate, CHIPS)
        for p in zeros:
            q_copy(p, g).start()
        q_copy(sibling, g).start()

    for copy in loads:
        copy.wait()

    def owner(i):
        return lax.rem(z + order(2 * lax.rem(i, CHIPS))[0], CHIPS) * 2 + 1 - i // CHIPS

    def chip_at(i):
        return lax.rem(z + order(2 * i)[0], CHIPS)

    def spread(row):
        wide = jnp.broadcast_to(row, (ROWS, ROWS))
        return wide, wide.T

    @pl.loop(0, GROUP)
    def _(i):
        p = owner(i)

        @pl.when(jnp.logical_or(
            jnp.logical_and(c == 0, p != g), jnp.logical_and(c == 1, lax.rem(p, 2) == 0)
        ))
        def _():
            level_copy(p, p).wait_recv()

        for h in range(2):
            _, down = spread(level_in[p, pl.ds(2 * c + h, 1), :])
            tail = jnp.exp(down[ROWS - 1 : ROWS, :] - down)
            scaled = (k_own[:, cols(p, h)].astype(F32) * tail).astype(BF16)
            state_own[p, h] = lax.dot_general(
                scaled, v_own[:, cols(p, h)], (((0,), (0,)), ((), ())),
                preferred_element_type=F32,
            )
        sib_copy(p).start()

    @pl.loop(0, GROUP)
    def _(i):
        sib_copy(owner(i)).wait_recv()

    for h in (KEPT, SENT):
        @pl.loop(0, CHIPS)
        def _(i):
            chip = chip_at(i)
            p = chip * 2 + c
            late = jnp.broadcast_to(level_in[p, 2 + h : 3 + h, ROWS - 1 : ROWS], (1, WIDTH))
            merged = (
                jnp.exp(late * (1.0 - cf)) * state_own[p, h]
                + jnp.exp(late * cf) * state_sib[p, h]
            )
            state_out[h, chip] = merged.astype(BF16)

            @pl.when(i < CHIPS - 1)
            def _():
                state_copy(h, chip, z).start()

            @pl.when(i == CHIPS - 1)
            def _():
                state_in[h, z] = state_out[h, z]

    causal = here >= there

    def inside(p, h):
        wide, down = spread(level_in[p, pl.ds(2 * c + h, 1), :])
        q_head = q_own[:, cols(p, h)]
        scores = lax.dot_general(
            q_head, k_own[:, cols(p, h)], (((1,), (1,)), ((), ())),
            preferred_element_type=F32,
        )
        gap = jnp.where(causal, down - wide, 0.0)
        weights = jnp.where(causal, scores * jnp.exp(gap), 0.0).astype(BF16)
        part = jnp.dot(weights, v_own[:, cols(p, h)], preferred_element_type=F32)
        scaled = (q_head.astype(F32) * (jnp.exp(down) * cf)).astype(BF16)
        return part + jnp.dot(
            scaled, state_sib[p, h].astype(BF16), preferred_element_type=F32
        )

    @pl.loop(0, GROUP)
    def _(i):
        p = peer(i)
        local_out[p] = inside(p, SENT).astype(BF16)

        @pl.when(i < GROUP - 1)
        def _():
            local_copy(p, g).start()

        @pl.when(i == GROUP - 1)
        def _():
            local_in[g] = local_out[g]

    @pl.loop(0, GROUP)
    def _(p):
        local_kept[p] = inside(p, KEPT)

    def chip_share(n, h):
        return jnp.exp(total[4 * n + h : 4 * n + h + 1, :] + total[4 * n + 2 + h : 4 * n + 3 + h, :])

    def send_block(h):
        @pl.loop(1, CHIPS)
        def _(d):
            chip = lax.rem(z + d, CHIPS)
            state_copy(h, chip, chip).wait_recv()

        run = state_in[h, 0].astype(F32)
        for n in range(1, CHIPS):
            run = chip_share(n, h) * run + state_in[h, n].astype(F32)
        block_out[h] = run.astype(BF16)
        for d in range(X_SIZE - 1):
            x_copy(h, d, x).start()
        x_state[h, x] = block_out[h, share(x), :]

    def send_row(h):
        for d in range(1, X_SIZE):
            x_copy(h, d - 1, lax.rem(x + d, X_SIZE)).wait_recv()
        run = x_state[h, 0].astype(F32)
        for n in range(1, X_SIZE):
            run = jnp.exp(x_total[n, 4 * h : 4 * h + 1, :]) * run + x_state[h, n].astype(F32)
        row_out[h] = run.astype(BF16)
        for d in range(Y_SIZE - 1):
            y_copy(h, d, y).start()
        y_state[h, y] = row_out[h]

    def cross(h):
        for d in range(Y_SIZE - 1):
            y_copy(h, d, lax.rem(y + d + 1, Y_SIZE)).wait_recv()
        run = jnp.zeros((SHARE, WIDTH), F32)
        for n in range(Y_SIZE - 1):
            used = (n < y).astype(F32)
            run = jnp.exp(y_total[n, 4 * h : 4 * h + 1, :] * used) * run + (
                y_state[h, n].astype(F32) * used
            )
        for n in range(X_SIZE):
            cross_out[h, n] = run
            run = jnp.exp(x_total[n, 4 * h : 4 * h + 1, :]) * run + x_state[h, n].astype(F32)
        for d in range(X_SIZE - 1):
            cross_copy(h, d, x).start()
        cross_in[h, x] = cross_out[h, x]

    def enter(h):
        for d in range(1, X_SIZE):
            cross_copy(h, d - 1, lax.rem(x + d, X_SIZE)).wait_recv()
        run = cross_in[h].reshape(WIDTH, WIDTH)
        for n in range(CHIPS):
            prefix[h, n] = run.astype(BF16)
            run = chip_share(n, h) * run + state_in[h, n].astype(F32)

    for d in range(1, X_SIZE):
        xt_copy(d - 1, lax.rem(x + d, X_SIZE)).wait_recv()
    for h in range(2):
        row_total = x_total[0, 4 * h : 4 * h + 1, :]
        for n in range(1, X_SIZE):
            row_total = row_total + x_total[n, 4 * h : 4 * h + 1, :]
        rowtot_out[4 * h : 4 * h + 4, :] = jnp.broadcast_to(row_total, (4, ROWS))
    for d in range(Y_SIZE - 1):
        yt_copy(d, y).start()
    y_total[y] = rowtot_out[...]

    send_block(KEPT)
    for d in range(Y_SIZE - 1):
        yt_copy(d, lax.rem(y + d + 1, Y_SIZE)).wait_recv()
    send_row(KEPT)
    send_block(SENT)
    cross(KEPT)
    enter(KEPT)

    @pl.loop(0, CHIPS - 1)
    def _(i):
        enter_copy(chip_at(i), g).start()

    entering[g] = prefix[KEPT, z]
    send_row(SENT)

    def finish_kept(p):
        row = level_in[p, pl.ds(2 * c + KEPT, 1), :] + cf * jnp.broadcast_to(
            level_in[p, KEPT : KEPT + 1, ROWS - 1 : ROWS], (1, ROWS)
        )
        _, down = spread(row)
        scaled = (q_own[:, cols(p, KEPT)].astype(F32) * jnp.exp(down)).astype(BF16)
        mixture = local_kept[p] + jnp.dot(scaled, entering[p], preferred_element_type=F32)
        mean_square = jnp.mean(mixture * mixture, axis=1, keepdims=True)
        normed = mixture * lax.rsqrt(mean_square + 1e-06) * level_in[p, 4:5, :]
        result_kept[p] = normed.astype(BF16)

    def own_done():
        return pltpu.make_async_copy(
            result_kept.at[g], out_hbm.at[rows(g), side(KEPT)], done_s.at[g]
        )

    pass_copy(g).start()

    @pl.loop(0, CHIPS - 1)
    def _(i):
        p = lax.rem(z + 2 * CHIPS - order(2 * i)[0], CHIPS) * 2 + c
        enter_copy(0, p).wait_recv()
        pass_copy(p).start()
        finish_kept(p)
        done_copy(p, g).start()

    cross(SENT)

    @pl.loop(0, CHIPS)
    def _(i):
        p = lax.rem(z + 2 * CHIPS - order(2 * i)[0], CHIPS) * 2 + 1 - c
        pass_copy(p).wait_recv()
        finish_kept(p)
        done_copy(p, g).start()

    finish_kept(g)
    own_done().start()

    enter(SENT)

    @pl.loop(0, GROUP - 1)
    def _(i):
        p = source(i)
        q_copy(p, p).wait_recv()

    @pl.loop(0, GROUP)
    def _(p):
        chip, core = p // 2, lax.rem(p, 2)
        row = level[pl.ds(2 * p + SENT, 1), :] + (
            core.astype(F32) * total[pl.ds(4 * chip + SENT, 1), :]
        )
        _, down = spread(row)
        scaled = (q_in[p].astype(F32) * jnp.exp(down)).astype(BF16)
        carried[p] = jnp.dot(scaled, prefix[SENT, chip], preferred_element_type=F32)

    def out_copy(p):
        return pltpu.make_async_copy(
            result.at[p], out_hbm.at[rows(p), side(SENT)], out_sem.at[p]
        )

    def finish_sent(p):
        mixture = carried[p] + local_in[p].astype(F32)
        mean_square = jnp.mean(mixture * mixture, axis=1, keepdims=True)
        normed = mixture * lax.rsqrt(mean_square + 1e-06) * gain_ref[:, 0:WIDTH]
        result[p] = normed.astype(BF16)
        out_copy(p).start()

    finish_sent(g)

    @pl.loop(0, GROUP - 1)
    def _(i):
        p = source(i)
        local_copy(p, p).wait_recv()
        finish_sent(p)

    @pl.loop(0, GROUP)
    def _(p):
        sib_copy(p).wait_send()

    @pl.loop(0, GROUP - 1)
    def _(i):
        p = peer(i)

        @pl.when(jnp.logical_or(c == 0, lax.rem(p, 2) == 1))
        def _():
            level_copy(p, g).wait_send()

        q_copy(p, g).wait_send()
        local_copy(p, g).wait_send()

    @pl.when(c == 1)
    def _():
        for n in range(CHIPS):
            hand_copy(2 * n + 1).wait_send()

    for h in range(2):
        @pl.loop(0, CHIPS - 1)
        def _(i):
            state_copy(h, chip_at(i), z).wait_send()

        for d in range(X_SIZE - 1):
            x_copy(h, d, x).wait_send()
            cross_copy(h, d, x).wait_send()
        for d in range(Y_SIZE - 1):
            y_copy(h, d, y).wait_send()

    @pl.loop(0, CHIPS - 1)
    def _(i):
        enter_copy(chip_at(i), g).wait_send()

    @pl.loop(0, CHIPS)
    def _(n):
        pass_copy(2 * n + c).wait_send()

    for d in range(X_SIZE - 1):
        xt_copy(d, x).wait_send()
    for d in range(Y_SIZE - 1):
        yt_copy(d, y).wait_send()
    own_done().wait()

    @pl.loop(0, GROUP)
    def _(p):
        out_copy(p).wait()

    @pl.loop(0, GROUP - 1)
    def _(i):
        p = source(i)
        done_copy(peer(i), g).wait_send()
        done_copy(p, p).wait_recv()


def local(queries, keys, values, log_decay, gain):
    chunk_decay = log_decay.reshape(2, GROUP, ROWS).transpose(1, 0, 2).reshape(2 * GROUP, ROWS)
    any_space = pl.BlockSpec(memory_space=pl.ANY)
    dma = pltpu.SemaphoreType.DMA
    own = pltpu.VMEM((ROWS, GROUP * 2 * WIDTH), BF16)
    tile = pltpu.VMEM((8, ROWS), F32)

    def parts(*lead):
        return pltpu.VMEM((*lead, ROWS, WIDTH), BF16)

    def wide_parts(*lead):
        return pltpu.VMEM((*lead, ROWS, WIDTH), F32)

    return pl.pallas_call(
        kernel,
        out_shape=jax.ShapeDtypeStruct((GROUP * ROWS, 2 * WIDTH), BF16),
        in_specs=[any_space] * 5,
        out_specs=any_space,
        scratch_shapes=[
            pltpu.VMEM((2 * GROUP, ROWS), F32),
            pltpu.VMEM((1, 2 * WIDTH), F32),
            own, own, own,
            pltpu.VMEM((2 * GROUP, ROWS), F32),
            pltpu.VMEM((2 * GROUP, ROWS), F32),
            pltpu.VMEM((CHIPS, 8, ROWS), F32),
            pltpu.VMEM((GROUP, 8, ROWS), F32),
            parts(GROUP),
            wide_parts(GROUP, 2), wide_parts(GROUP, 2),
            parts(2, CHIPS), parts(2, CHIPS),
            parts(GROUP), parts(GROUP), wide_parts(GROUP),
            parts(2), pltpu.VMEM((2, X_SIZE, SHARE, WIDTH), BF16),
            pltpu.VMEM((X_SIZE, 8, ROWS), F32),
            pltpu.VMEM((2, SHARE, WIDTH), BF16), pltpu.VMEM((2, Y_SIZE, SHARE, WIDTH), BF16),
            pltpu.VMEM((Y_SIZE, 8, ROWS), F32),
            tile, tile,
            pltpu.VMEM((2, X_SIZE, SHARE, WIDTH), F32), pltpu.VMEM((2, X_SIZE, SHARE, WIDTH), F32),
            parts(2, CHIPS), parts(GROUP), wide_parts(GROUP), parts(GROUP), parts(GROUP),
            dma((6,)),
            dma((GROUP,)), dma((GROUP,)),
            dma((GROUP,)), dma((GROUP,)),
            dma((GROUP,)), dma((GROUP,)),
            dma((2, CHIPS)), dma((2, CHIPS)),
            dma((GROUP,)), dma((GROUP,)),
            dma((2, X_SIZE)), dma((2, X_SIZE)), dma((X_SIZE,)), dma((X_SIZE,)),
            dma((2, Y_SIZE)), dma((2, Y_SIZE)), dma((Y_SIZE,)), dma((Y_SIZE,)),
            dma((2, X_SIZE)), dma((2, X_SIZE)),
            dma((CHIPS,)), dma((GROUP,)), dma((GROUP,)), dma((GROUP,)), dma((GROUP,)),
            dma((GROUP,)), dma((GROUP,)),
            pltpu.SemaphoreType.REGULAR, pltpu.SemaphoreType.REGULAR,
        ],
        compiler_params=pltpu.CompilerParams(
            collective_id=0, has_side_effects=True, vmem_limit_bytes=60 << 20
        ),
    )(queries, keys, values, chunk_decay, gain.reshape(1, 2 * WIDTH))


def solution(mesh):
    return jax.shard_map(
        local,
        mesh=mesh,
        in_specs=(
            P(("seq", "grp"), None), P(("seq", "grp"), None), P(("seq", "grp"), None),
            P("grp", "seq"), P("grp"),
        ),
        out_specs=P("seq", "grp"),
        check_vma=False,
    )
```
